512 devices in a mesh: layer: 4 (over x), expert: 128 (over z, y, core).
Axes of the slice: x: 4, y: 8, z: 8, core: 2. Of those that a mesh axis runs over, the one named last changes fastest.
Arguments:
- rows: bfloat16 [65536, 2048], P(('layer', 'expert')), parts along dimension 0, may hold values from -6 to 6
- expert_ids: int32 [65536, 8], P(('layer', 'expert')), parts along dimension 0, may hold values from 0 to 127, all different within a row; in each aligned block of 128 rows (0 to 127, 128 to 255, ...) at most 10 rows name the same one
- start_basis: float32 [8192, 128], P(('layer', 'expert')), parts along dimension 0, may hold values from -6 to 6
- weights: bfloat16 [512, 768, 2048], P(('layer', 'expert')), parts along dimension 0, may hold values from -0.125 to 0.125
Outputs:
- compressed: bfloat16 [512, 768, 128], P(('layer', 'expert')), parts along dimension 0
- basis: float32 [8192, 128], P(('layer', 'expert')), parts along dimension 0
The draws below stay inside these ranges and needn't reach their ends.
There are 4 independent parts, one for each index of `layer`. The reference program is written for one: setup_inputs(seed, part) draws one part's arguments, and reference() takes and returns one part's arrays. A program takes and returns all parts, laid end to end along the dimension named above; each array names one. Nothing has to cross between parts.
Inputs may be any that keep to these rules, and one draw needn't show every extreme that they name: `expert_ids`: each row names 8 different experts; among the 128 rows of one device no expert is named by more than 10 rows, a bound that some blocks reach.
All inputs are finite; a program needn't handle non-finite values.
Results may differ from the reference program's by a relative error of at most 0.0075.
Values may be sent and summed in bfloat16 or wider, within the bound.
No kernel may reach another device: no remote copies, remote signals or barrier semaphores. Data moves between devices by JAX's collectives and lax.ppermute only.
A program may use at most 64 MiB of HBM per device.

```python
import math
import jax
import jax.numpy as jnp
import numpy as np
from jax import lax

D = 2048
FF = 768
TOP = 8
R = 128
NS_STEPS = 3
TOK_DEV = 128
EXPERTS = 128
TOKENS = 16384
CAP = 10
N_EXPERT = 128


def levels(own_key, dims, cuts, least, largest):
    factor_of, own = 1.0, jax.random.fold_in(own_key, 6)
    for axis_at, blocks in cuts:
        steps = jnp.exp(jax.random.uniform(jax.random.fold_in(own, axis_at), (blocks,), jnp.float32, least / len(cuts), largest / len(cuts)))
        factor_of = factor_of * jnp.repeat(steps, dims[axis_at] // blocks).reshape([-1 if axis == axis_at else 1 for axis in range(len(dims))])
    return factor_of


def shared_out(stream_key, own, number, rows, number_of, top, bound, skew):
    sequence = jax.random.permutation(stream_key, number_of)
    crowded, usual = shares(number_of, rows * top, bound, skew, True), shares(number_of, rows * top, bound, skew, False)
    places = jnp.arange(number_of)

    def named(sizes, rotation):
        used = int((sizes > 0).sum())
        fixed = max(1, used // 4)
        passed = fixed + (places - fixed + rotation * (used - fixed)) % max(1, number_of - fixed)
        return jnp.zeros((number_of,), jnp.int32).at[sequence[jnp.where(places < fixed, places, passed)]].set(jnp.asarray(sizes, jnp.int32))

    sizes = jnp.where(number % 4 == 0, named(crowded, number // 4), named(usual, number - number // 4 - 1))
    mixed = jax.random.permutation(jax.random.fold_in(own, 3), number_of)
    source_of, taker = mixed[0:number_of // 2 * 2:2], mixed[1:number_of // 2 * 2:2]
    margin = jnp.minimum(sizes[source_of] - 1, bound - sizes[taker]) // 2
    margin = jnp.where((source_of == sequence[0]) | (taker == sequence[0]) | (sizes[taker] == 0), 0, jnp.maximum(margin, 0))
    passed = jax.random.randint(jax.random.fold_in(own, 4), (number_of // 2,), 0, 1 << 20) % (margin + 1)
    sizes = sizes.at[source_of].add(-passed).at[taker].add(passed)
    labels = jnp.searchsorted(jnp.cumsum(sizes), jnp.arange(rows * top), side="right").astype(jnp.int32)
    grid = labels.reshape(top, rows).T
    grid = grid[jax.random.permutation(jax.random.fold_in(own, 1), rows)]
    rotation = jax.random.randint(jax.random.fold_in(own, 2), (rows, 1), 0, top)
    return jnp.take_along_axis(grid, (jnp.arange(top)[None, :] + rotation) % top, axis=1)


def shares(amount, total, reach, skew, full):
    weights = [(1 << 20) // math.isqrt(grade ** skew) + 1 for grade in range(1, amount + 1)]
    largest = reach if full else min(reach, max(-(-total // amount), total * weights[0] // sum(weights)))
    least = 1 if total - largest >= amount - 1 else 0
    given, spare = [largest] + [least] * (amount - 1), total - largest - least * (amount - 1)
    while spare > 0:
        movable = [i for i in range(1, amount) if given[i] < largest] or [i for i in range(1, amount) if given[i] < reach]
        mass, budget = sum([weights[i] for i in movable]), spare
        for i in movable:
            addition = min(reach - given[i], max(1, budget * weights[i] // mass), spare)
            given[i] = given[i] + addition
            spare = spare - addition
    return np.array(given)


def scatter_about(key, extent, spread, most, split=(), kind=jnp.bfloat16):
    level = levels(key, extent, split, -0.22, 0.18) if split else 1.0
    values = jax.random.normal(key, extent, jnp.float32) * spread * level
    return jnp.minimum(jnp.maximum(values, -most), most).astype(kind)


def setup_inputs(seed: int = 0, part: int = 0) -> dict:
    key_list = jax.random.split(jax.random.key(seed), 5)
    own_keys = jax.random.split(jax.random.fold_in(key_list[4], part), 5)
    rows = scatter_about(own_keys[0], (TOKENS, D), 1.0, 6.0, ((0, 128),))
    expert_ids_keys = jax.random.split(jax.random.fold_in(own_keys[1], 1), TOKENS // TOK_DEV)
    expert_ids_turns = jax.random.permutation(jax.random.fold_in(own_keys[1], 3), TOKENS // TOK_DEV)
    expert_ids = jax.vmap(lambda own, number: shared_out(jax.random.fold_in(own_keys[1], 2), own, number, TOK_DEV, EXPERTS, TOP, CAP, 2))(expert_ids_keys, expert_ids_turns).reshape((TOKENS, TOP))
    start_basis = scatter_about(own_keys[2], (D, R), 1.0, 6.0, ((0, 128),), jnp.float32)
    weights = scatter_about(own_keys[3], (EXPERTS, FF, D), D ** -0.5, 0.125, ((0, 128),))
    return dict(rows=rows, expert_ids=expert_ids, start_basis=start_basis, weights=weights)


epsilon = 1e-06
coef_a = 3.4445
coef_b = -4.775
coef_c = 2.0315

def normalize(rows):
    values = rows.astype(jnp.float32)
    power = lax.optimization_barrier(jnp.mean(values * values, axis=1, keepdims=True)) + epsilon
    return (values / jnp.sqrt(power)).astype(jnp.bfloat16)

def slot_table(block_ids):
    flat_ids = block_ids.reshape(-1).astype(jnp.int32)
    onehot = (flat_ids[:, None] == jnp.arange(EXPERTS, dtype=jnp.int32)[None, :]).astype(jnp.int32)
    before = jnp.cumsum(onehot, axis=0) - onehot
    slot_rank = lax.optimization_barrier(jnp.sum(before * onehot, axis=1)).astype(jnp.int32)
    position = (flat_ids * CAP + slot_rank).astype(jnp.int32)
    source_row = jnp.arange(flat_ids.shape[0], dtype=jnp.int32) // TOP
    empty = jnp.full((EXPERTS * CAP,), TOK_DEV, jnp.int32)
    return empty.at[position].set(source_row.astype(jnp.int32))

def ortho_whole(total):
    power = jnp.sum(total * total) + epsilon
    current = total / jnp.sqrt(power)
    for inner_step in range(NS_STEPS):
        gram = jnp.dot(current.T, current, precision=lax.Precision.HIGHEST)
        square = jnp.dot(gram, gram, precision=lax.Precision.HIGHEST)
        current = coef_a * current + jnp.dot(current, coef_b * gram + coef_c * square, precision=lax.Precision.HIGHEST)
    return current

def reference(rows, expert_ids, start_basis, weights):
    normed = normalize(rows)
    padded = jnp.concatenate([normed, jnp.zeros((1, D), jnp.bfloat16)], axis=0)
    blocks = expert_ids.reshape(N_EXPERT, TOK_DEV, TOP)
    tables = jax.vmap(slot_table)(blocks)
    offsets = (jnp.arange(N_EXPERT, dtype=jnp.int32) * TOK_DEV)[:, None]
    global_rows = jnp.where(tables < TOK_DEV, tables + offsets, TOKENS).astype(jnp.int32)
    per_expert = global_rows.reshape(N_EXPERT, EXPERTS, CAP).transpose(1, 0, 2).reshape(EXPERTS, N_EXPERT * CAP)
    basis_bf = start_basis.astype(jnp.bfloat16)

    def expert_term(carry, inputs):
        index_rows, weight = inputs
        gathered = padded[index_rows]
        first = jnp.dot(gathered, basis_bf, preferred_element_type=jnp.float32).astype(jnp.bfloat16)
        second = jnp.dot(gathered.T, first, preferred_element_type=jnp.float32).astype(jnp.bfloat16)
        inner = jnp.dot(weight, second, preferred_element_type=jnp.float32).astype(jnp.bfloat16)
        back = jnp.dot(weight.T, inner, preferred_element_type=jnp.float32).astype(jnp.bfloat16)
        again = jnp.dot(gathered, back, preferred_element_type=jnp.float32).astype(jnp.bfloat16)
        return (carry + jnp.dot(gathered.T, again, preferred_element_type=jnp.float32), None)
    total, unused = lax.scan(expert_term, jnp.zeros((D, R), jnp.float32), (per_expert, weights))
    current = ortho_whole(total)
    final_bf = current.astype(jnp.bfloat16)
    compressed = jnp.einsum('efd,dr->efr', weights.astype(jnp.float32), final_bf.astype(jnp.float32)).astype(jnp.bfloat16)
    return (compressed, current)
```

```python
import jax
import jax.numpy as jnp
from jax import lax
from jax.sharding import PartitionSpec as P

NS_STEPS = 3
MAIN = 8

epsilon = 1e-06
coef_a = 3.4445
coef_b = -4.775
coef_c = 2.0315
HI = lax.Precision.HIGHEST


def dot(a, b):
    return jnp.dot(a, b, preferred_element_type=jnp.float32)


def dot_t(a, b):
    return lax.dot_general(a, b, (((0,), (0,)), ((), ())), preferred_element_type=jnp.float32)


def slot_rank(block_ids, experts):
    row_count = block_ids.shape[0]
    names = jnp.arange(experts, dtype=jnp.int32)[:, None, None]
    member = jnp.any(block_ids[None, :, :] == names, axis=2).astype(jnp.bfloat16)
    index = jnp.arange(row_count, dtype=jnp.int32)
    ahead = (index[:, None] <= index[None, :]).astype(jnp.bfloat16)
    rank = jnp.dot(member, ahead, preferred_element_type=jnp.float32)
    return jnp.where(member > 0, rank, 0.0)


def pick(rank, normed, first, count):
    wanted = jnp.arange(first + 1, first + count + 1).astype(jnp.float32)
    chosen = (rank[:, None, :] == wanted[None, :, None]).astype(jnp.bfloat16)
    chosen = chosen.reshape(rank.shape[0] * count, rank.shape[1])
    return dot(chosen, normed).astype(jnp.bfloat16)


def ortho(total, own):
    power = jnp.sum(total * total) + epsilon
    scale = 1.0 / jnp.sqrt(power)
    current = total * scale
    eye = jnp.eye(total.shape[1], dtype=jnp.float32)
    gram = jnp.dot(current.T, current, precision=HI)
    product = None
    for step in range(NS_STEPS):
        square = jnp.dot(gram, gram, precision=HI)
        factor = coef_a * eye + coef_b * gram + coef_c * square
        product = factor if product is None else jnp.dot(product, factor, precision=HI)
        if step + 1 < NS_STEPS:
            gram = jnp.dot(jnp.dot(factor, gram, precision=HI), factor, precision=HI)
    return jnp.dot(current, product, precision=HI), jnp.dot(own * scale, product, precision=HI)


def shards(rows, expert_ids, start_basis, weights):
    row_count, width = rows.shape
    rank_width = start_basis.shape[1]
    share = start_basis.shape[0]
    group = lax.axis_size("expert")
    experts = group * weights.shape[0]
    capacity = max(2, min(row_count, row_count * expert_ids.shape[1] * 5 // (4 * experts)))
    spare = capacity - MAIN
    weight = weights[0]
    values = rows.astype(jnp.float32)
    power = jnp.mean(values * values, axis=1, keepdims=True) + epsilon
    normed = (values / jnp.sqrt(power)).astype(jnp.bfloat16)
    rank = slot_rank(expert_ids, experts)
    main = pick(rank, normed, 0, MAIN).reshape(experts, MAIN, width)
    rest = pick(rank, normed, MAIN, spare).reshape(experts, spare * width // rank_width, rank_width)
    basis_rows = jnp.broadcast_to(start_basis.astype(jnp.bfloat16), (experts, share, rank_width))
    second = jnp.concatenate([rest, basis_rows], axis=1)
    second = lax.all_to_all(second, "expert", split_axis=0, concat_axis=0, tiled=True)
    main = lax.all_to_all(main, "expert", split_axis=0, concat_axis=0, tiled=True)
    cut = spare * width // rank_width
    basis_bf = second[:, cut:, :].reshape(group * share, rank_width)
    x_rest = second[:, :cut, :].reshape(group * spare, width)
    x_main = main.reshape(group * MAIN, width)
    bf = jnp.bfloat16
    a_main = dot(x_main, basis_bf).astype(bf)
    a_rest = dot(x_rest, basis_bf).astype(bf)
    b = (dot_t(x_main, a_main) + dot_t(x_rest, a_rest)).astype(bf)
    c = dot(weight, b).astype(bf)
    e = dot_t(weight, c).astype(bf)
    f_main = dot(x_main, e).astype(bf)
    f_rest = dot(x_rest, e).astype(bf)
    term = dot_t(x_main, f_main) + dot_t(x_rest, f_rest)
    parts = lax.all_to_all(term.reshape(group, share, rank_width), "expert", split_axis=0, concat_axis=0, tiled=True)
    own = jnp.sum(parts, axis=0)
    spread = jnp.broadcast_to(own[None], (group, share, rank_width))
    total = lax.all_to_all(spread, "expert", split_axis=0, concat_axis=0, tiled=True).reshape(group * share, rank_width)
    whole, local = ortho(total, own)
    compressed = dot(weight, whole.astype(bf)).astype(bf)
    return (compressed[None], local)


def solution(mesh):
    in_specs = (
        P(("layer", "expert"), None),
        P(("layer", "expert"), None),
        P(("layer", "expert"), None),
        P(("layer", "expert"), None, None),
    )
    out_specs = (P(("layer", "expert"), None, None), P(("layer", "expert"), None))
    return jax.shard_map(shards, mesh=mesh, in_specs=in_specs, out_specs=out_specs, check_vma=False)
```

```python
import jax
import jax.numpy as jnp
from jax import lax
from jax.experimental import pallas as pl
from jax.experimental.pallas import tpu as pltpu
from jax.sharding import Mesh, PartitionSpec as P

NS_STEPS = 3
MAIN = 8
LANES = 128
STEP = 16

epsilon = 1e-06
coef_a = 3.4445
coef_b = -4.775
coef_c = 2.0315
HI = lax.Precision.HIGHEST
BF = jnp.bfloat16
F32 = jnp.float32


def iota(shape, axis):
    return lax.broadcasted_iota(jnp.int32, shape, axis)


def dot(a, b, contract=((1,), (0,)), precision=None):
    return lax.dot_general(a, b, (contract, ((), ())), precision=precision, preferred_element_type=F32)


def as_bf16(flag):
    return jnp.where(flag, 1.0, 0.0).astype(BF)


def pack_kernel(main_steps, spare, ids_ref, rows_ref, basis_ref, out_ref, normed_ref, rank_ref, pick_ref, fan_ref):
    step = pl.program_id(0)
    tops, row_count = ids_ref.shape
    experts = out_ref.shape[0]

    @pl.when(step == 0)
    def _():
        values = rows_ref[...].astype(F32)
        power = jnp.mean(values * values, axis=1, keepdims=True) + epsilon
        normed = (values / jnp.sqrt(power)).astype(BF)
        for t in range(main_steps):
            normed_ref[t] = normed[:, 2 * LANES * t:2 * LANES * (t + 1)]
        member = jnp.zeros((experts, row_count), F32)
        for top in range(tops):
            named = jnp.broadcast_to(ids_ref[top:top + 1, :], (experts, row_count))
            member = member + jnp.where(named == iota((experts, row_count), 0), 1.0, 0.0)
        ahead = as_bf16(iota((row_count, row_count), 0) <= iota((row_count, row_count), 1))
        rank = jnp.where(member > 0.0, dot(member.astype(BF), ahead), 0.0)
        rank_ref[...] = rank
        slots = experts * MAIN
        owner = as_bf16(iota((slots, experts), 0) // MAIN == iota((slots, experts), 1))
        wanted = (iota((slots, row_count), 0) % MAIN + 1).astype(F32)
        pick_ref[...] = as_bf16(dot(owner, rank.astype(BF)) == wanted)

    @pl.when(step < main_steps)
    def _():
        both = dot(pick_ref[...], normed_ref[step]).astype(BF)
        out_ref[:, 0:MAIN, :] = both[:, :LANES].reshape(experts, MAIN, LANES)
        out_ref[:, MAIN:, :] = both[:, LANES:].reshape(experts, MAIN, LANES)

    @pl.when((step >= main_steps) & (step < main_steps + spare))
    def _():
        wanted = (step - main_steps + MAIN + 1).astype(F32)
        pick = as_bf16(rank_ref[...] == wanted)
        for t in range(main_steps):
            both = dot(pick, normed_ref[t])
            fan_ref[pl.ds(2 * t, experts, stride=STEP), :] = both[:, :LANES]
            fan_ref[pl.ds(2 * t + 1, experts, stride=STEP), :] = both[:, LANES:]
        out_ref[...] = fan_ref[...].reshape(experts, STEP, LANES).astype(BF)

    @pl.when(step == main_steps + spare)
    def _():
        basis = basis_ref[...].astype(BF)
        out_ref[...] = jnp.broadcast_to(basis[None], out_ref.shape)


def pack(ids_t, rows, basis, experts, spare):
    row_count, width = rows.shape
    main_steps = width // (2 * LANES)
    steps = main_steps + spare + 1
    return pl.pallas_call(
        lambda *refs: pack_kernel(main_steps, spare, *refs),
        grid=(steps,),
        out_shape=jax.ShapeDtypeStruct((experts, STEP * steps, LANES), BF),
        in_specs=[
            pl.BlockSpec(ids_t.shape, lambda i: (0, 0)),
            pl.BlockSpec(rows.shape, lambda i: (0, 0)),
            pl.BlockSpec(basis.shape, lambda i: (0, 0)),
        ],
        out_specs=pl.BlockSpec((experts, STEP, LANES), lambda i: (0, i, 0)),
        scratch_shapes=[
            pltpu.VMEM((main_steps, row_count, 2 * LANES), BF),
            pltpu.VMEM((experts, row_count), F32),
            pltpu.VMEM((experts * MAIN, row_count), BF),
            pltpu.VMEM((experts * STEP, LANES), F32),
        ],
        name="pack",
    )(ids_t, rows, basis)


def chain_kernel(main_steps, spare, core_ref, got_ref, weight_ref, keep_ref, send_ref, buf, x, w, fan, y, sems, w_sem):
    steps = main_steps + spare + 1
    group = got_ref.shape[0]
    core = core_ref[0]
    copies = [
        pltpu.make_async_copy(got_ref.at[:, pl.ds(STEP * i, STEP), :], buf.at[i], sems.at[i]) for i in range(steps)
    ]
    load_w = pltpu.make_async_copy(weight_ref, w, w_sem)
    order = [steps - 1] + list(range(main_steps, main_steps + spare)) + list(range(main_steps))
    for i in order:
        copies[i].start()
    load_w.start()
    copies[steps - 1].wait()
    basis = buf[steps - 1].reshape(group * STEP, LANES)
    main = group * MAIN
    for k in range(spare):
        copies[main_steps + k].wait()
        fan[...] = buf[main_steps + k].reshape(group * STEP, LANES).astype(F32)
        for j in range(STEP):
            x[pl.ds(main + group * k, group), LANES * j:LANES * (j + 1)] = fan[
                pl.ds(j, group, stride=STEP), :
            ].astype(BF)
    first = None
    for t in range(main_steps):
        copies[t].wait()
        at = 2 * LANES * t
        x[0:main, at:at + LANES] = buf[t, :, 0:MAIN, :].reshape(main, LANES)
        x[0:main, at + LANES:at + 2 * LANES] = buf[t, :, MAIN:, :].reshape(main, LANES)
        part = dot(x[:, at:at + 2 * LANES], basis[at:at + 2 * LANES, :])
        first = part if first is None else first + part
    rows = x[...]
    second = dot(first.astype(BF), rows, ((0,), (0,))).astype(BF)
    load_w.wait()
    weight = w[...]
    inner = dot(second, weight, ((1,), (1,))).astype(BF)
    back = dot(inner, weight).astype(BF)
    again = dot(rows, back, ((1,), (1,))).astype(BF)
    term = dot(again, rows, ((0,), (0,)))
    y[...] = term.T.reshape(y.shape)
    keep_ref[...] = y[:, core]
    send_ref[...] = y[:, 1 - core]


def chain(core, got, weight, spare):
    group = got.shape[0]
    width = weight.shape[1]
    main_steps = width // (2 * LANES)
    steps = main_steps + spare + 1
    half = jax.ShapeDtypeStruct((group // 2, STEP, LANES), F32)
    vmem = pl.BlockSpec(memory_space=pltpu.VMEM)
    hbm = pl.BlockSpec(memory_space=pl.ANY)
    return pl.pallas_call(
        lambda *refs: chain_kernel(main_steps, spare, *refs),
        out_shape=(half, half),
        in_specs=[pl.BlockSpec(memory_space=pltpu.SMEM), hbm, hbm],
        out_specs=(vmem, vmem),
        scratch_shapes=[
            pltpu.VMEM((steps, group, STEP, LANES), BF),
            pltpu.VMEM((group * (MAIN + spare), width), BF),
            pltpu.VMEM(weight.shape, BF),
            pltpu.VMEM((group * STEP, LANES), F32),
            pltpu.VMEM((group // 2, 2, STEP, LANES), F32),
            pltpu.SemaphoreType.DMA((steps,)),
            pltpu.SemaphoreType.DMA,
        ],
        name="chain",
    )(core, got, weight)


def ortho_kernel(core_ref, mine_ref, other_ref, own_ref, weight_ref, packed_ref, local_ref, z, w, w_sem):
    core = core_ref[0]
    load_w = pltpu.make_async_copy(weight_ref, w, w_sem)
    load_w.start()
    z[:, core] = mine_ref[...]
    z[:, 1 - core] = other_ref[...]
    size = z.shape[0] * z.shape[1] * z.shape[2]
    total = z[...].reshape(size, LANES)
    raw = dot(total, total, ((0,), (0,)), HI)
    diagonal = iota((LANES, LANES), 0) == iota((LANES, LANES), 1)
    eye = jnp.where(diagonal, 1.0, 0.0)
    power = jnp.sum(jnp.where(diagonal, raw, 0.0), keepdims=True) + epsilon
    scale = 1.0 / jnp.sqrt(power)
    gram = (raw * scale) * scale
    product = None
    for step in range(NS_STEPS):
        factor = coef_a * eye + coef_b * gram + coef_c * dot(gram, gram, precision=HI)
        product = factor if product is None else dot(product, factor, precision=HI)
        if step + 1 < NS_STEPS:
            gram = dot(dot(factor, gram, precision=HI), factor, precision=HI)
    whole = dot(total * scale, product, precision=HI)
    local_ref[...] = dot(own_ref[...] * scale, product, precision=HI)
    load_w.wait()
    packed_ref[...] = dot(w[...], whole.astype(BF)).astype(BF)


def ortho(core, mine, other, own, weight):
    vmem = pl.BlockSpec(memory_space=pltpu.VMEM)
    return pl.pallas_call(
        ortho_kernel,
        out_shape=(
            jax.ShapeDtypeStruct((weight.shape[0], LANES), BF),
            jax.ShapeDtypeStruct(own.shape, F32),
        ),
        in_specs=[pl.BlockSpec(memory_space=pltpu.SMEM), vmem, vmem, vmem, pl.BlockSpec(memory_space=pl.ANY)],
        out_specs=(vmem, vmem),
        scratch_shapes=[
            pltpu.VMEM((mine.shape[0], 2) + mine.shape[1:], F32),
            pltpu.VMEM(weight.shape, BF),
            pltpu.SemaphoreType.DMA,
        ],
        name="ortho",
    )(core, mine, other, own, weight)


def shards(rows, expert_ids, start_basis, weights):
    row_count = rows.shape[0]
    experts = lax.axis_size("chip") * lax.axis_size("core") * weights.shape[0]
    capacity = max(2, min(row_count, row_count * expert_ids.shape[1] * 5 // (4 * experts)))
    spare = capacity - MAIN
    weight = weights[0]
    core = lax.axis_index("core").astype(jnp.int32).reshape(1)
    swap = [(0, 1), (1, 0)]
    sent = pack(expert_ids.T, rows, start_basis, experts, spare)
    got = lax.all_to_all(sent, ("chip", "core"), split_axis=0, concat_axis=0, tiled=True)
    keep, send = chain(core, got, weight, spare)
    half = keep + lax.ppermute(send, "core", swap)
    parts = lax.all_to_all(half, "chip", split_axis=0, concat_axis=0, tiled=True)
    own = jnp.sum(parts, axis=0)
    spread = jnp.broadcast_to(own[None], parts.shape)
    mine = lax.all_to_all(spread, "chip", split_axis=0, concat_axis=0, tiled=True)
    other = lax.ppermute(mine, "core", swap)
    compressed, local = ortho(core, mine, other, own, weight)
    return (compressed[None], local)


def solution(mesh):
    layers, members = mesh.devices.shape
    inner = Mesh(mesh.devices.reshape(layers, members // 2, 2), ("layer", "chip", "core"))
    split = ("layer", "chip", "core")
    in_specs = (P(split, None), P(split, None), P(split, None), P(split, None, None))
    out_specs = (P(split, None, None), P(split, None))
    return jax.shard_map(shards, mesh=inner, in_specs=in_specs, out_specs=out_specs, check_vma=False)
```

```python
import jax
import jax.numpy as jnp
from jax import lax
from jax.experimental import pallas as pl
from jax.experimental.pallas import tpu as pltpu
from jax.sharding import Mesh, PartitionSpec as P

NS_STEPS = 3
MAIN = 8
LANES = 128
STEP = 16

epsilon = 1e-06
coef_a = 3.4445
coef_b = -4.775
coef_c = 2.0315
HI = lax.Precision.HIGHEST
BF = jnp.bfloat16
F32 = jnp.float32


def iota(shape, axis):
    return lax.broadcasted_iota(jnp.int32, shape, axis)


def dot(a, b, contract=((1,), (0,)), precision=None):
    return lax.dot_general(a, b, (contract, ((), ())), precision=precision, preferred_element_type=F32)


def as_bf16(flag):
    return jnp.where(flag, 1.0, 0.0).astype(BF)


def pack_kernel(main_steps, spare, ids_ref, rows_ref, basis_ref, out_ref, buf, fan, sems):
    tops, row_count = ids_ref.shape
    experts = out_ref.shape[0]
    steps = main_steps + spare + 1
    copies = [
        pltpu.make_async_copy(buf.at[i], out_ref.at[:, pl.ds(STEP * i, STEP), :], sems.at[i]) for i in range(steps)
    ]
    buf[steps - 1] = jnp.broadcast_to(basis_ref[...].astype(BF)[None], (experts, STEP, LANES))
    copies[steps - 1].start()
    values = rows_ref[...].astype(F32)
    power = jnp.mean(values * values, axis=1, keepdims=True) + epsilon
    normed = (values / jnp.sqrt(power)).astype(BF)
    member = jnp.zeros((experts, row_count), F32)
    for top in range(tops):
        named = jnp.broadcast_to(ids_ref[top:top + 1, :], (experts, row_count))
        member = member + jnp.where(named == iota((experts, row_count), 0), 1.0, 0.0)
    ahead = as_bf16(iota((row_count, row_count), 0) <= iota((row_count, row_count), 1))
    rank = jnp.where(member > 0.0, dot(member.astype(BF), ahead), 0.0)
    slots = experts * MAIN
    owner = as_bf16(iota((slots, experts), 0) // MAIN == iota((slots, experts), 1))
    wanted = (iota((slots, row_count), 0) % MAIN + 1).astype(F32)
    pick = as_bf16(dot(owner, rank.astype(BF)) == wanted)
    for t in range(main_steps):
        both = dot(pick, normed[:, 2 * LANES * t:2 * LANES * (t + 1)]).astype(BF)
        buf[t, :, 0:MAIN, :] = both[:, :LANES].reshape(experts, MAIN, LANES)
        buf[t, :, MAIN:, :] = both[:, LANES:].reshape(experts, MAIN, LANES)
        copies[t].start()
    for k in range(spare):
        late = as_bf16(rank == MAIN + k + 1.0)
        for t in range(main_steps):
            both = dot(late, normed[:, 2 * LANES * t:2 * LANES * (t + 1)])
            fan[k, pl.ds(2 * t, experts, stride=STEP), :] = both[:, :LANES]
            fan[k, pl.ds(2 * t + 1, experts, stride=STEP), :] = both[:, LANES:]
        buf[main_steps + k] = fan[k].reshape(experts, STEP, LANES).astype(BF)
        copies[main_steps + k].start()
    for copy in copies:
        copy.wait()


def pack(ids_t, rows, basis, experts, spare):
    main_steps = rows.shape[1] // (2 * LANES)
    steps = main_steps + spare + 1
    vmem = pl.BlockSpec(memory_space=pltpu.VMEM)
    return pl.pallas_call(
        lambda *refs: pack_kernel(main_steps, spare, *refs),
        out_shape=jax.ShapeDtypeStruct((experts, STEP * steps, LANES), BF),
        in_specs=[vmem, vmem, vmem],
        out_specs=pl.BlockSpec(memory_space=pl.ANY),
        scratch_shapes=[
            pltpu.VMEM((steps, experts, STEP, LANES), BF),
            pltpu.VMEM((spare, experts * STEP, LANES), F32),
            pltpu.SemaphoreType.DMA((steps,)),
        ],
        name="pack",
    )(ids_t, rows, basis)


def chain_kernel(main_steps, spare, core_ref, got_ref, weight_ref, keep_ref, send_ref, buf, x, w, fan, y, sems, w_sem):
    steps = main_steps + spare + 1
    group = got_ref.shape[0]
    core = core_ref[0]
    copies = [
        pltpu.make_async_copy(got_ref.at[:, pl.ds(STEP * i, STEP), :], buf.at[i], sems.at[i]) for i in range(steps)
    ]
    load_w = pltpu.make_async_copy(weight_ref, w, w_sem)
    order = [steps - 1] + list(range(main_steps, main_steps + spare)) + list(range(main_steps))
    for i in order:
        copies[i].start()
    load_w.start()
    copies[steps - 1].wait()
    basis = buf[steps - 1].reshape(group * STEP, LANES)
    main = group * MAIN
    for k in range(spare):
        copies[main_steps + k].wait()
        fan[...] = buf[main_steps + k].reshape(group * STEP, LANES).astype(F32)
        for j in range(STEP):
            x[pl.ds(main + group * k, group), LANES * j:LANES * (j + 1)] = fan[
                pl.ds(j, group, stride=STEP), :
            ].astype(BF)
    first = None
    for t in range(main_steps):
        copies[t].wait()
        at = 2 * LANES * t
        x[0:main, at:at + LANES] = buf[t, :, 0:MAIN, :].reshape(main, LANES)
        x[0:main, at + LANES:at + 2 * LANES] = buf[t, :, MAIN:, :].reshape(main, LANES)
    rows = x[...]
    first = dot(basis, rows, ((0,), (1,)))
    second = dot(first.astype(BF), rows).astype(BF)
    load_w.wait()
    weight = w[...]
    inner = dot(second, weight, ((1,), (1,))).astype(BF)
    back = dot(inner, weight).astype(BF)
    again = dot(back, rows, ((1,), (1,))).astype(BF)
    term = dot(again, rows)
    y[...] = term.T.reshape(y.shape)
    keep_ref[...] = y[:, core]
    send_ref[...] = y[:, 1 - core]


def chain(core, got, weight, spare):
    group = got.shape[0]
    width = weight.shape[1]
    main_steps = width // (2 * LANES)
    steps = main_steps + spare + 1
    half = jax.ShapeDtypeStruct((group // 2, STEP, LANES), F32)
    vmem = pl.BlockSpec(memory_space=pltpu.VMEM)
    hbm = pl.BlockSpec(memory_space=pl.ANY)
    return pl.pallas_call(
        lambda *refs: chain_kernel(main_steps, spare, *refs),
        out_shape=(half, half),
        in_specs=[pl.BlockSpec(memory_space=pltpu.SMEM), hbm, hbm],
        out_specs=(vmem, vmem),
        scratch_shapes=[
            pltpu.VMEM((steps, group, STEP, LANES), BF),
            pltpu.VMEM((group * (MAIN + spare), width), BF),
            pltpu.VMEM(weight.shape, BF),
            pltpu.VMEM((group * STEP, LANES), F32),
            pltpu.VMEM((group // 2, 2, STEP, LANES), F32),
            pltpu.SemaphoreType.DMA((steps,)),
            pltpu.SemaphoreType.DMA,
        ],
        name="chain",
    )(core, got, weight)


def ortho_kernel(core_ref, mine_ref, other_ref, own_ref, weight_ref, packed_ref, local_ref, z, w, w_sem):
    core = core_ref[0]
    load_w = pltpu.make_async_copy(weight_ref, w, w_sem)
    load_w.start()
    size = z.shape[0] * STEP
    mine = mine_ref[...].reshape(size, LANES)
    other = other_ref[...].reshape(size, LANES)
    raw = dot(mine, mine, ((0,), (0,)), HI) + dot(other, other, ((0,), (0,)), HI)
    diagonal = iota((LANES, LANES), 0) == iota((LANES, LANES), 1)
    eye = jnp.where(diagonal, 1.0, 0.0)
    power = jnp.sum(jnp.where(diagonal, raw, 0.0), keepdims=True) + epsilon
    scale = 1.0 / jnp.sqrt(power)
    gram = (raw * scale) * scale
    product = None
    for step in range(NS_STEPS):
        factor = coef_a * eye + coef_b * gram + coef_c * dot(gram, gram, precision=HI)
        product = factor if product is None else dot(product, factor, precision=HI)
        if step + 1 < NS_STEPS:
            gram = dot(dot(factor, gram, precision=HI), factor, precision=HI)
    final = product * scale
    z[:, core] = dot(mine, final, precision=HI).astype(BF).reshape(mine_ref.shape)
    z[:, 1 - core] = dot(other, final, precision=HI).astype(BF).reshape(mine_ref.shape)
    local_ref[...] = dot(own_ref[...], final, precision=HI)
    load_w.wait()
    packed_ref[...] = dot(w[...], z[...].reshape(2 * size, LANES)).astype(BF)


def ortho(core, mine, other, own, weight):
    vmem = pl.BlockSpec(memory_space=pltpu.VMEM)
    return pl.pallas_call(
        ortho_kernel,
        out_shape=(
            jax.ShapeDtypeStruct((weight.shape[0], LANES), BF),
            jax.ShapeDtypeStruct(own.shape, F32),
        ),
        in_specs=[pl.BlockSpec(memory_space=pltpu.SMEM), vmem, vmem, vmem, pl.BlockSpec(memory_space=pl.ANY)],
        out_specs=(vmem, vmem),
        scratch_shapes=[
            pltpu.VMEM((mine.shape[0], 2) + mine.shape[1:], BF),
            pltpu.VMEM(weight.shape, BF),
            pltpu.SemaphoreType.DMA,
        ],
        name="ortho",
    )(core, mine, other, own, weight)


def shards(rows, expert_ids, start_basis, weights):
    row_count = rows.shape[0]
    experts = lax.axis_size("chip") * lax.axis_size("core") * weights.shape[0]
    capacity = max(2, min(row_count, row_count * expert_ids.shape[1] * 5 // (4 * experts)))
    spare = capacity - MAIN
    weight = weights[0]
    core = lax.axis_index("core").astype(jnp.int32).reshape(1)
    swap = [(0, 1), (1, 0)]
    sent = pack(expert_ids.T, rows, start_basis, experts, spare)
    got = lax.all_to_all(sent, ("chip", "core"), split_axis=0, concat_axis=0, tiled=True)
    keep, send = chain(core, got, weight, spare)
    half = keep + lax.ppermute(send, "core", swap)
    parts = lax.all_to_all(half, "chip", split_axis=0, concat_axis=0, tiled=True)
    own = jnp.sum(parts, axis=0)
    spread = jnp.broadcast_to(own[None], parts.shape)
    mine = lax.all_to_all(spread, "chip", split_axis=0, concat_axis=0, tiled=True)
    other = lax.ppermute(mine, "core", swap)
    compressed, local = ortho(core, mine, other, own, weight)
    return (compressed[None], local)


def solution(mesh):
    layers, members = mesh.devices.shape
    inner = Mesh(mesh.devices.reshape(layers, members // 2, 2), ("layer", "chip", "core"))
    split = ("layer", "chip", "core")
    in_specs = (P(split, None), P(split, None), P(split, None), P(split, None, None))
    out_specs = (P(split, None, None), P(split, None))
    return jax.shard_map(shards, mesh=inner, in_specs=in_specs, out_specs=out_specs, check_vma=False)
```

```python
import jax
import jax.numpy as jnp
from jax import lax
from jax.experimental import pallas as pl
from jax.experimental.pallas import tpu as pltpu
from jax.sharding import Mesh, PartitionSpec as P

NS_STEPS = 3
MAIN = 8
LANES = 128
STEP = 16

epsilon = 1e-06
coef_a = 3.4445
coef_b = -4.775
coef_c = 2.0315
HI = lax.Precision.HIGHEST
BF = jnp.bfloat16
F32 = jnp.float32


def iota(shape, axis):
    return lax.broadcasted_iota(jnp.int32, shape, axis)


def dot(a, b, contract=((1,), (0,)), precision=None):
    return lax.dot_general(a, b, (contract, ((), ())), precision=precision, preferred_element_type=F32)


def as_bf16(flag):
    return jnp.where(flag, 1.0, 0.0).astype(BF)


def pack_kernel(main_steps, spare, side_ref, ids_ref, rows_ref, basis_ref, *rest):
    out_ref, buf, fan, sems = rest[-4:]
    core, slot = side_ref[0], side_ref[1]
    tops, row_count = ids_ref.shape
    chips = out_ref.shape[0]
    steps = main_steps + spare + 1
    copies = [pltpu.make_async_copy(buf.at[i], out_ref.at[:, 2 * i + slot], sems.at[i]) for i in range(steps)]
    buf[steps - 1] = jnp.broadcast_to(basis_ref[...][None], (chips, STEP, LANES))
    copies[steps - 1].start()
    values = rows_ref[...].astype(F32)
    power = jnp.mean(values * values, axis=1, keepdims=True) + epsilon
    normed = (values / jnp.sqrt(power)).astype(BF)
    owner_names = (2 * iota((chips, row_count), 0) + core).astype(F32)
    member = jnp.zeros((chips, row_count), F32)
    for top in range(tops):
        named = jnp.broadcast_to(ids_ref[top:top + 1, :].astype(F32), (chips, row_count))
        member = member + jnp.where(named == owner_names, 1.0, 0.0)
    ahead = as_bf16(iota((row_count, row_count), 0) <= iota((row_count, row_count), 1))
    rank = jnp.where(member > 0.0, dot(member.astype(BF), ahead), 0.0)
    slots = chips * MAIN
    owner = as_bf16(iota((slots, chips), 0) // MAIN == iota((slots, chips), 1))
    wanted = (iota((slots, row_count), 0) % MAIN + 1).astype(F32)
    pick = as_bf16(dot(owner, rank.astype(BF)) == wanted)
    for t in range(main_steps):
        both = dot(pick, normed[:, 2 * LANES * t:2 * LANES * (t + 1)]).astype(BF)
        buf[t, :, 0:MAIN, :] = both[:, :LANES].reshape(chips, MAIN, LANES)
        buf[t, :, MAIN:, :] = both[:, LANES:].reshape(chips, MAIN, LANES)
        copies[t].start()
    for k in range(spare):
        late = as_bf16(rank == MAIN + k + 1.0)
        for t in range(main_steps):
            both = dot(late, normed[:, 2 * LANES * t:2 * LANES * (t + 1)])
            fan[k, pl.ds(2 * t, chips, stride=STEP), :] = both[:, :LANES]
            fan[k, pl.ds(2 * t + 1, chips, stride=STEP), :] = both[:, LANES:]
        buf[main_steps + k] = fan[k].reshape(chips, STEP, LANES).astype(BF)
        copies[main_steps + k].start()
    for copy in copies:
        copy.wait()


def pack(side, ids, rows, basis, filled, chips, spare):
    main_steps = rows.shape[1] // (2 * LANES)
    steps = main_steps + spare + 1
    vmem = pl.BlockSpec(memory_space=pltpu.VMEM)
    hbm = pl.BlockSpec(memory_space=pl.ANY)
    return pl.pallas_call(
        lambda *refs: pack_kernel(main_steps, spare, *refs),
        out_shape=jax.ShapeDtypeStruct((chips, 2 * steps, STEP, LANES), BF),
        in_specs=[pl.BlockSpec(memory_space=pltpu.SMEM), vmem, vmem, vmem] + [hbm] * len(filled),
        out_specs=hbm,
        scratch_shapes=[
            pltpu.VMEM((steps, chips, STEP, LANES), BF),
            pltpu.VMEM((spare, chips * STEP, LANES), F32),
            pltpu.SemaphoreType.DMA((steps,)),
        ],
        input_output_aliases={4: 0} if filled else {},
        cost_estimate=pl.CostEstimate(flops=400_000_000, bytes_accessed=4_000_000, transcendentals=0),
        name="pack",
    )(side, ids, rows, basis, *filled)


def chain_kernel(main_steps, spare, core_ref, got_ref, weight_ref, keep_ref, send_ref, buf, x, w, fan, y, sems, w_sem):
    steps = main_steps + spare + 1
    group = 2 * got_ref.shape[0]
    core = core_ref[0]
    copies = [
        pltpu.make_async_copy(got_ref.at[:, pl.ds(2 * i, 2)], buf.at[i], sems.at[i]) for i in range(steps)
    ]
    load_w = pltpu.make_async_copy(weight_ref, w, w_sem)
    order = [steps - 1] + list(range(main_steps, main_steps + spare)) + list(range(main_steps))
    for i in order:
        copies[i].start()
    load_w.start()
    copies[steps - 1].wait()
    basis = buf[steps - 1].reshape(group * STEP, LANES)
    main = group * MAIN
    for k in range(spare):
        copies[main_steps + k].wait()
        fan[...] = buf[main_steps + k].reshape(group * STEP, LANES).astype(F32)
        for j in range(STEP):
            x[pl.ds(main + group * k, group), LANES * j:LANES * (j + 1)] = fan[
                pl.ds(j, group, stride=STEP), :
            ].astype(BF)
    first = None
    for t in range(main_steps):
        copies[t].wait()
        at = 2 * LANES * t
        x[0:main, at:at + LANES] = buf[t, :, :, 0:MAIN, :].reshape(main, LANES)
        x[0:main, at + LANES:at + 2 * LANES] = buf[t, :, :, MAIN:, :].reshape(main, LANES)
    rows = x[...]
    first = dot(basis, rows, ((0,), (1,)))
    second = dot(first.astype(BF), rows).astype(BF)
    load_w.wait()
    weight = w[...]
    inner = dot(second, weight, ((1,), (1,))).astype(BF)
    back = dot(inner, weight).astype(BF)
    again = dot(back, rows, ((1,), (1,))).astype(BF)
    term = dot(again, rows)
    y[...] = term.T.reshape(y.shape)
    keep_ref[...] = y[:, core]
    send_ref[...] = y[:, 1 - core]


def chain(core, got, weight, spare):
    group = 2 * got.shape[0]
    width = weight.shape[1]
    main_steps = width // (2 * LANES)
    steps = main_steps + spare + 1
    half = jax.ShapeDtypeStruct((group // 2, STEP, LANES), F32)
    vmem = pl.BlockSpec(memory_space=pltpu.VMEM)
    hbm = pl.BlockSpec(memory_space=pl.ANY)
    return pl.pallas_call(
        lambda *refs: chain_kernel(main_steps, spare, *refs),
        out_shape=(half, half),
        in_specs=[pl.BlockSpec(memory_space=pltpu.SMEM), hbm, hbm],
        out_specs=(vmem, vmem),
        scratch_shapes=[
            pltpu.VMEM((steps, group // 2, 2, STEP, LANES), BF),
            pltpu.VMEM((group * (MAIN + spare), width), BF),
            pltpu.VMEM(weight.shape, BF),
            pltpu.VMEM((group * STEP, LANES), F32),
            pltpu.VMEM((group // 2, 2, STEP, LANES), F32),
            pltpu.SemaphoreType.DMA((steps,)),
            pltpu.SemaphoreType.DMA,
        ],
        name="chain",
    )(core, got, weight)


def ortho_kernel(core_ref, mine_ref, other_ref, own_ref, weight_ref, packed_ref, local_ref, z, w, w_sem):
    core = core_ref[0]
    load_w = pltpu.make_async_copy(weight_ref, w, w_sem)
    load_w.start()
    size = z.shape[0] * STEP
    mine = mine_ref[...].reshape(size, LANES)
    other = other_ref[...].reshape(size, LANES)
    raw = dot(mine, mine, ((0,), (0,)), HI) + dot(other, other, ((0,), (0,)), HI)
    diagonal = iota((LANES, LANES), 0) == iota((LANES, LANES), 1)
    eye = jnp.where(diagonal, 1.0, 0.0)
    power = jnp.sum(jnp.where(diagonal, raw, 0.0), keepdims=True) + epsilon
    scale = 1.0 / jnp.sqrt(power)
    gram = (raw * scale) * scale
    product = None
    for step in range(NS_STEPS):
        factor = coef_a * eye + coef_b * gram + coef_c * dot(gram, gram, precision=HI)
        product = factor if product is None else dot(product, factor, precision=HI)
        if step + 1 < NS_STEPS:
            gram = dot(dot(factor, gram, precision=HI), factor, precision=HI)
    final = product * scale
    z[:, core] = dot(mine, final, precision=HI).astype(BF).reshape(mine_ref.shape)
    z[:, 1 - core] = dot(other, final, precision=HI).astype(BF).reshape(mine_ref.shape)
    local_ref[...] = dot(own_ref[...], final, precision=HI)
    load_w.wait()
    packed_ref[...] = dot(w[...], z[...].reshape(2 * size, LANES)).astype(BF)


def ortho(core, mine, other, own, weight):
    vmem = pl.BlockSpec(memory_space=pltpu.VMEM)
    return pl.pallas_call(
        ortho_kernel,
        out_shape=(
            jax.ShapeDtypeStruct((weight.shape[0], LANES), BF),
            jax.ShapeDtypeStruct(own.shape, F32),
        ),
        in_specs=[pl.BlockSpec(memory_space=pltpu.SMEM), vmem, vmem, vmem, pl.BlockSpec(memory_space=pl.ANY)],
        out_specs=(vmem, vmem),
        scratch_shapes=[
            pltpu.VMEM((mine.shape[0], 2) + mine.shape[1:], BF),
            pltpu.VMEM(weight.shape, BF),
            pltpu.SemaphoreType.DMA,
        ],
        name="ortho",
    )(core, mine, other, own, weight)


def shards(rows, expert_ids, start_basis, weights):
    row_count = rows.shape[0]
    experts = lax.axis_size("chip") * lax.axis_size("core") * weights.shape[0]
    capacity = max(2, min(row_count, row_count * expert_ids.shape[1] * 5 // (4 * experts)))
    spare = capacity - MAIN
    weight = weights[0]
    chips = experts // 2
    core = lax.axis_index("core").astype(jnp.int32).reshape(1)
    swap = [(0, 1), (1, 0)]
    tops = expert_ids.shape[1]
    small = jnp.concatenate([expert_ids.T.astype(BF), start_basis.astype(BF)], axis=0)
    rows_there = lax.ppermute(rows, "core", swap)
    small_there = lax.ppermute(small, "core", swap)
    here = jnp.concatenate([core, core])
    there = jnp.concatenate([core, 1 - core])
    sent = pack(here, small[:tops], rows, small[tops:], (), chips, spare)
    sent = pack(there, small_there[:tops], rows_there, small_there[tops:], (sent,), chips, spare)
    got = lax.all_to_all(sent, "chip", split_axis=0, concat_axis=0, tiled=True)
    keep, send = chain(core, got, weight, spare)
    half = keep + lax.ppermute(send, "core", swap)
    parts = lax.all_to_all(half, "chip", split_axis=0, concat_axis=0, tiled=True)
    own = jnp.sum(parts, axis=0)
    spread = jnp.broadcast_to(own[None], parts.shape)
    mine = lax.all_to_all(spread, "chip", split_axis=0, concat_axis=0, tiled=True)
    other = lax.ppermute(mine, "core", swap)
    compressed, local = ortho(core, mine, other, own, weight)
    return (compressed[None], local)


def solution(mesh):
    layers, members = mesh.devices.shape
    inner = Mesh(mesh.devices.reshape(layers, members // 2, 2), ("layer", "chip", "core"))
    split = ("layer", "chip", "core")
    in_specs = (P(split, None), P(split, None), P(split, None), P(split, None, None))
    out_specs = (P(split, None, None), P(split, None))
    return jax.shard_map(shards, mesh=inner, in_specs=in_specs, out_specs=out_specs, check_vma=False)
```

```python
import jax
import jax.numpy as jnp
from jax import lax
from jax.experimental import pallas as pl
from jax.experimental.pallas import tpu as pltpu
from jax.sharding import Mesh, PartitionSpec as P

NS_STEPS = 3
MAIN = 8
LANES = 128
STEP = 16

epsilon = 1e-06
coef_a = 3.4445
coef_b = -4.775
coef_c = 2.0315
HI = lax.Precision.HIGHEST
BF = jnp.bfloat16
F32 = jnp.float32


def iota(shape, axis):
    return lax.broadcasted_iota(jnp.int32, shape, axis)


def dot(a, b, contract=((1,), (0,)), precision=None):
    return lax.dot_general(a, b, (contract, ((), ())), precision=precision, preferred_element_type=F32)


def as_bf16(flag):
    return jnp.where(flag, 1.0, 0.0).astype(BF)


def pack_kernel(main_steps, spare, mirrored, core_ref, small_ref, rows_ref, *rest):
    out_ref, buf, fan, sems = rest[-4:]
    core = core_ref[0]
    slot = 1 - core if mirrored else core
    tops = small_ref.shape[0] - STEP
    row_count = rows_ref.shape[0]
    chips = out_ref.shape[0]
    steps = main_steps + spare + 1
    copies = [pltpu.make_async_copy(buf.at[i], out_ref.at[:, 2 * i + slot], sems.at[i]) for i in range(steps)]
    buf[steps - 1] = jnp.broadcast_to(small_ref[tops:, :].astype(BF)[None], (chips, STEP, LANES))
    copies[steps - 1].start()
    values = rows_ref[...].astype(F32)
    power = jnp.mean(values * values, axis=1, keepdims=True) + epsilon
    normed = (values / jnp.sqrt(power)).astype(BF)
    owner_names = (2 * iota((chips, row_count), 0) + core).astype(F32)
    member = jnp.zeros((chips, row_count), F32)
    for top in range(tops):
        named = jnp.broadcast_to(small_ref[top:top + 1, :], (chips, row_count))
        member = member + jnp.where(named == owner_names, 1.0, 0.0)
    ahead = as_bf16(iota((row_count, row_count), 0) <= iota((row_count, row_count), 1))
    rank = jnp.where(member > 0.0, dot(member.astype(BF), ahead), 0.0)
    slots = chips * MAIN
    owner = as_bf16(iota((slots, chips), 0) // MAIN == iota((slots, chips), 1))
    wanted = (iota((slots, row_count), 0) % MAIN + 1).astype(F32)
    pick = as_bf16(dot(owner, rank.astype(BF)) == wanted)
    for t in range(main_steps):
        both = dot(pick, normed[:, 2 * LANES * t:2 * LANES * (t + 1)]).astype(BF)
        buf[t, :, 0:MAIN, :] = both[:, :LANES].reshape(chips, MAIN, LANES)
        buf[t, :, MAIN:, :] = both[:, LANES:].reshape(chips, MAIN, LANES)
        copies[t].start()
    for k in range(spare):
        late = as_bf16(rank == MAIN + k + 1.0)
        for t in range(main_steps):
            both = dot(late, normed[:, 2 * LANES * t:2 * LANES * (t + 1)])
            fan[k, pl.ds(2 * t, chips, stride=STEP), :] = both[:, :LANES]
            fan[k, pl.ds(2 * t + 1, chips, stride=STEP), :] = both[:, LANES:]
        buf[main_steps + k] = fan[k].reshape(chips, STEP, LANES).astype(BF)
        copies[main_steps + k].start()
    for copy in copies:
        copy.wait()


def pack(core, small, rows, filled, chips, spare):
    main_steps = rows.shape[1] // (2 * LANES)
    steps = main_steps + spare + 1
    vmem = pl.BlockSpec(memory_space=pltpu.VMEM)
    hbm = pl.BlockSpec(memory_space=pl.ANY)
    return pl.pallas_call(
        lambda *refs: pack_kernel(main_steps, spare, bool(filled), *refs),
        out_shape=jax.ShapeDtypeStruct((chips, 2 * steps, STEP, LANES), BF),
        in_specs=[pl.BlockSpec(memory_space=pltpu.SMEM), vmem, vmem] + [hbm] * len(filled),
        out_specs=hbm,
        scratch_shapes=[
            pltpu.VMEM((steps, chips, STEP, LANES), BF),
            pltpu.VMEM((spare, chips * STEP, LANES), F32),
            pltpu.SemaphoreType.DMA((steps,)),
        ],
        input_output_aliases={3: 0} if filled else {},
        cost_estimate=pl.CostEstimate(flops=400_000_000, bytes_accessed=4_000_000, transcendentals=0),
        name="pack",
    )(core, small, rows, *filled)


def chain_kernel(main_steps, spare, core_ref, got_ref, weight_ref, keep_ref, send_ref, buf, x, w, fan, y, sems, w_sem):
    steps = main_steps + spare + 1
    group = 2 * got_ref.shape[0]
    core = core_ref[0]
    copies = [
        pltpu.make_async_copy(got_ref.at[:, pl.ds(2 * i, 2)], buf.at[i], sems.at[i]) for i in range(steps)
    ]
    load_w = pltpu.make_async_copy(weight_ref, w, w_sem)
    order = [steps - 1] + list(range(main_steps, main_steps + spare)) + list(range(main_steps))
    for i in order:
        copies[i].start()
    load_w.start()
    copies[steps - 1].wait()
    basis = buf[steps - 1].reshape(group * STEP, LANES)
    main = group * MAIN
    for k in range(spare):
        copies[main_steps + k].wait()
        fan[...] = buf[main_steps + k].reshape(group * STEP, LANES).astype(F32)
        for j in range(STEP):
            x[pl.ds(main + group * k, group), LANES * j:LANES * (j + 1)] = fan[
                pl.ds(j, group, stride=STEP), :
            ].astype(BF)
    first = None
    for t in range(main_steps):
        copies[t].wait()
        at = 2 * LANES * t
        x[0:main, at:at + LANES] = buf[t, :, :, 0:MAIN, :].reshape(main, LANES)
        x[0:main, at + LANES:at + 2 * LANES] = buf[t, :, :, MAIN:, :].reshape(main, LANES)
    rows = x[...]
    first = dot(basis, rows, ((0,), (1,)))
    second = dot(first.astype(BF), rows).astype(BF)
    load_w.wait()
    weight = w[...]
    inner = dot(second, weight, ((1,), (1,))).astype(BF)
    back = dot(inner, weight).astype(BF)
    again = dot(back, rows, ((1,), (1,))).astype(BF)
    term = dot(again, rows)
    y[...] = term.T.reshape(y.shape)
    keep_ref[...] = y[:, core]
    send_ref[...] = y[:, 1 - core]


def chain(core, got, weight, spare):
    group = 2 * got.shape[0]
    width = weight.shape[1]
    main_steps = width // (2 * LANES)
    steps = main_steps + spare + 1
    half = jax.ShapeDtypeStruct((group // 2, STEP, LANES), F32)
    vmem = pl.BlockSpec(memory_space=pltpu.VMEM)
    hbm = pl.BlockSpec(memory_space=pl.ANY)
    return pl.pallas_call(
        lambda *refs: chain_kernel(main_steps, spare, *refs),
        out_shape=(half, half),
        in_specs=[pl.BlockSpec(memory_space=pltpu.SMEM), hbm, hbm],
        out_specs=(vmem, vmem),
        scratch_shapes=[
            pltpu.VMEM((steps, group // 2, 2, STEP, LANES), BF),
            pltpu.VMEM((group * (MAIN + spare), width), BF),
            pltpu.VMEM(weight.shape, BF),
            pltpu.VMEM((group * STEP, LANES), F32),
            pltpu.VMEM((group // 2, 2, STEP, LANES), F32),
            pltpu.SemaphoreType.DMA((steps,)),
            pltpu.SemaphoreType.DMA,
        ],
        name="chain",
    )(core, got, weight)


def ortho_kernel(core_ref, mine_ref, other_ref, own_ref, weight_ref, packed_ref, local_ref, z, w, w_sem):
    core = core_ref[0]
    load_w = pltpu.make_async_copy(weight_ref, w, w_sem)
    load_w.start()
    size = z.shape[0] * STEP
    mine = mine_ref[...].reshape(size, LANES)
    other = other_ref[...].reshape(size, LANES)
    raw = dot(mine, mine, ((0,), (0,)), HI) + dot(other, other, ((0,), (0,)), HI)
    diagonal = iota((LANES, LANES), 0) == iota((LANES, LANES), 1)
    eye = jnp.where(diagonal, 1.0, 0.0)
    power = jnp.sum(jnp.where(diagonal, raw, 0.0), keepdims=True) + epsilon
    scale = 1.0 / jnp.sqrt(power)
    gram = (raw * scale) * scale
    product = None
    for step in range(NS_STEPS):
        factor = coef_a * eye + coef_b * gram + coef_c * dot(gram, gram, precision=HI)
        product = factor if product is None else dot(product, factor, precision=HI)
        if step + 1 < NS_STEPS:
            gram = dot(dot(factor, gram, precision=HI), factor, precision=HI)
    final = product * scale
    z[:, core] = dot(mine, final, precision=HI).astype(BF).reshape(mine_ref.shape)
    z[:, 1 - core] = dot(other, final, precision=HI).astype(BF).reshape(mine_ref.shape)
    local_ref[...] = dot(own_ref[...], final, precision=HI)
    load_w.wait()
    packed_ref[...] = dot(w[...], z[...].reshape(2 * size, LANES)).astype(BF)


def ortho(core, mine, other, own, weight):
    vmem = pl.BlockSpec(memory_space=pltpu.VMEM)
    return pl.pallas_call(
        ortho_kernel,
        out_shape=(
            jax.ShapeDtypeStruct((weight.shape[0], LANES), BF),
            jax.ShapeDtypeStruct(own.shape, F32),
        ),
        in_specs=[pl.BlockSpec(memory_space=pltpu.SMEM), vmem, vmem, vmem, pl.BlockSpec(memory_space=pl.ANY)],
        out_specs=(vmem, vmem),
        scratch_shapes=[
            pltpu.VMEM((mine.shape[0], 2) + mine.shape[1:], BF),
            pltpu.VMEM(weight.shape, BF),
            pltpu.SemaphoreType.DMA,
        ],
        name="ortho",
    )(core, mine, other, own, weight)


def shards(rows, expert_ids, start_basis, weights):
    row_count = rows.shape[0]
    experts = lax.axis_size("chip") * lax.axis_size("core") * weights.shape[0]
    capacity = max(2, min(row_count, row_count * expert_ids.shape[1] * 5 // (4 * experts)))
    spare = capacity - MAIN
    weight = weights[0]
    chips = experts // 2
    core = lax.axis_index("core").astype(jnp.int32).reshape(1)
    swap = [(0, 1), (1, 0)]
    small = jnp.concatenate([expert_ids.T.astype(F32), start_basis], axis=0)
    rows_there = lax.ppermute(rows, "core", swap)
    small_there = lax.ppermute(small, "core", swap)
    sent = pack(core, small, rows, (), chips, spare)
    sent = pack(core, small_there, rows_there, (sent,), chips, spare)
    got = lax.all_to_all(sent, "chip", split_axis=0, concat_axis=0, tiled=True)
    keep, send = chain(core, got, weight, spare)
    half = keep + lax.ppermute(send, "core", swap)
    parts = lax.all_to_all(half, "chip", split_axis=0, concat_axis=0, tiled=True)
    own = jnp.sum(parts, axis=0)
    spread = jnp.broadcast_to(own[None], parts.shape)
    mine = lax.all_to_all(spread, "chip", split_axis=0, concat_axis=0, tiled=True)
    other = lax.ppermute(mine, "core", swap)
    compressed, local = ortho(core, mine, other, own, weight)
    return (compressed[None], local)


def solution(mesh):
    layers, members = mesh.devices.shape
    inner = Mesh(mesh.devices.reshape(layers, members // 2, 2), ("layer", "chip", "core"))
    split = ("layer", "chip", "core")
    in_specs = (P(split, None), P(split, None), P(split, None), P(split, None, None))
    out_specs = (P(split, None, None), P(split, None))
    return jax.shard_map(shards, mesh=inner, in_specs=in_specs, out_specs=out_specs, check_vma=False)
```
